32 devices in a mesh: tm: 16 (over z, y, x), tile: 2 (over core).
Axes of the slice: x: 2, y: 2, z: 4, core: 2. Of those that a mesh axis runs over, the one named last changes fastest.
Arguments:
- prior_space: float32 [1536, 1536], P('tile'), as said below
- node_gain: float32 [1536], replicated, may hold values from 0.4 to 1
- time_diag: float32 [32], P('tm'), may hold values from 0.6 to 1.5
- rho: float32 [32], P('tm'), may hold values from 0.2 to 0.95
- obs_values: float32 [2, 512, 16, 768], P('tile', 'tm'), may hold values from -1 to 1
- obs_weight: float32 [2, 512, 16], P('tile', 'tm'), may hold values from 0.25 to 4
- obs_step: int32 [2, 16, 32], P('tile', 'tm'), may hold values from 0 to 31, each once within a row
Outputs:
- separator_block: float32 [16, 1536, 1536], P('tm', 'tile')
- separator_coupling: float32 [16, 1536, 1536], P('tm', 'tile')
- interior_logdet: float32 [16], P('tm')
The draws below stay inside these ranges and needn't reach their ends.
Inputs may be any that keep to these rules, and one draw needn't show every extreme that they name: prior_space is symmetric and each diagonal entry exceeds the sum of magnitudes of the other entries of its row. For each node block c and each index m of tm, obs_step[c, m] names every time step exactly once.
All inputs are finite; a program needn't handle non-finite values.
Results may differ from the reference program's by a relative error of at most 0.00013.
Values sent between devices are 32-bit elements; how exact they have to be, the bound alone decides.
A program may use at most 192 MiB of HBM per device.

```python
import math
import jax
import jax.numpy as jnp
from jax import lax

NODES = 1536
OBS_BLK = 16
BLOCK = 768
STEPS = 32
OBS_DEV = 32
N_TM = 16
N_TILE = 2


def draw_prior_space(key, part):
    key_mod, key_diag = jax.random.split(key, 2)
    strength = 4.0
    reach = NODES / 64.0
    bound_total = 2.0 / (math.exp(1.0 / reach) - 1.0)
    order = jnp.arange(NODES, dtype=jnp.float32)
    modulate = jax.random.uniform(key_mod, (NODES, NODES), jnp.float32, 0.8, 1.0)
    symmetric = 0.5 * (modulate + modulate.T)
    distance = jnp.abs(order[:, None] - order[None, :])
    off_part = -(strength / bound_total) * jnp.exp(-distance / reach) * symmetric
    diag_vals = strength * jax.random.uniform(key_diag, (NODES,), jnp.float32, 1.02, 1.25)
    row_ids = lax.broadcasted_iota(jnp.int32, (NODES, NODES), 0)
    col_ids = lax.broadcasted_iota(jnp.int32, (NODES, NODES), 1)
    return jnp.where(row_ids == col_ids, diag_vals[:, None] * jnp.ones((1, NODES), jnp.float32), off_part)


def level_of(key, dims, cuts, least, top_value):
    level, own = 1.0, jax.random.fold_in(key, 6)
    for axis_at, blocks in cuts:
        draws = jnp.exp(jax.random.uniform(jax.random.fold_in(own, axis_at), (blocks,), jnp.float32, least / len(cuts), top_value / len(cuts)))
        level = level * jnp.repeat(draws, dims[axis_at] // blocks).reshape([-1 if axis == axis_at else 1 for axis in range(len(dims))])
    return level


def centred(stream_key, extent, width, limit, shards=(), kind=jnp.bfloat16):
    array = width * jax.random.normal(stream_key, extent, jnp.float32)
    if shards:
        array = array * level_of(stream_key, extent, shards, -0.22, 0.18)
    return jnp.clip(array, -limit, limit).astype(kind)


def setup_inputs(seed: int = 0) -> dict:
    key_list = jax.random.split(jax.random.key(seed), 8)
    prior_space = draw_prior_space(jax.random.fold_in(key_list[7], 71), 0)
    node_gain = jnp.clip(jax.random.uniform(key_list[1], (NODES,), jnp.float32, 0.4, 1.0), 0.4, 1.0)
    time_diag = jnp.clip(jnp.exp(math.log(1.5) - 0.9162907 * jax.random.uniform(key_list[2], (STEPS,), jnp.float32) ** level_of(key_list[2], (STEPS,), ((0, 16),), -0.2, 0.2)), 0.6, 1.5)
    rho = jnp.clip(0.2 + 0.75 * jax.random.uniform(key_list[3], (STEPS,), jnp.float32) ** level_of(key_list[3], (STEPS,), ((0, 16),), -0.2, 0.2), 0.2, 0.95)
    obs_values = centred(key_list[4], (N_TILE, N_TM * OBS_DEV, OBS_BLK, BLOCK), (1.0 / (N_TM * OBS_BLK) ** 0.5), 1.0, ((0, 2), (1, 16)), jnp.float32)
    obs_weight = jnp.clip(jnp.exp(math.log(4.0) - 2.7725887 * jax.random.uniform(key_list[5], (N_TILE, N_TM * OBS_DEV, OBS_BLK), jnp.float32) ** level_of(key_list[5], (N_TILE, N_TM * OBS_DEV, OBS_BLK), ((0, 2), (1, 16)), -0.2, 0.2)), 0.25, 4.0)
    obs_step = jax.vmap(lambda own: jax.random.permutation(own, STEPS))(jax.random.split(key_list[6], N_TILE * N_TM)).reshape((N_TILE, N_TM, STEPS)).astype(jnp.int32)
    return {"prior_space": prior_space, "node_gain": node_gain, "time_diag": time_diag, "rho": rho, "obs_values": obs_values, "obs_weight": obs_weight, "obs_step": obs_step}


def reference(prior_space, node_gain, time_diag, rho, obs_values, obs_weight, obs_step):
    precise = lax.Precision.HIGHEST
    scaled = obs_values * obs_weight[..., None]
    tile_steps = obs_step.reshape(N_TILE, N_TM * OBS_DEV)

    def add_tile(grams, inputs):
        scaled_tile, plain_tile, step_ids = inputs
        terms = jnp.einsum('crb,crd->cbd', scaled_tile, plain_tile, precision=precise)

        def place(gram_block, step_id, term_block):
            current = lax.dynamic_index_in_dim(gram_block, step_id, 0, keepdims=False)
            return lax.dynamic_update_index_in_dim(gram_block, current + term_block, step_id, 0)
        return (jax.vmap(place)(grams, step_ids, terms), None)
    start_grams = jnp.zeros((N_TILE, STEPS, BLOCK, BLOCK), jnp.float32)
    grams, unused = lax.scan(add_tile, start_grams, (jnp.swapaxes(scaled, 0, 1), jnp.swapaxes(obs_values, 0, 1), jnp.swapaxes(tile_steps, 0, 1)))
    grams = jnp.transpose(grams.reshape(N_TILE, N_TM, 2, BLOCK, BLOCK), (1, 2, 0, 3, 4))
    picker = jnp.eye(N_TILE, dtype=jnp.float32)

    def assemble(coef, gram_step):
        placed = gram_step[:, :, None, :] * picker[:, None, :, None]
        return coef * prior_space + placed.reshape(NODES, NODES)
    coefs = time_diag.reshape(N_TM, 2)
    rates = rho.reshape(N_TM, 2)
    gain_matrix = jnp.diag(node_gain)

    def interior(inputs):
        coef, gram_step = inputs
        matrix = assemble(coef, gram_step)
        lower_factor = jnp.linalg.cholesky(matrix)
        log_det = 2.0 * jnp.sum(jnp.log(jnp.diagonal(lower_factor))) / NODES
        half_solve = lax.linalg.triangular_solve(lower_factor, gain_matrix, left_side=True, lower=True)
        inverse_cols = lax.linalg.triangular_solve(lower_factor, half_solve, left_side=True, lower=True, transpose_a=True)
        return (node_gain[:, None] * inverse_cols, log_det)
    schur_all, interior_logdet = lax.map(interior, (coefs[:, 0], grams[:, 0]))
    shifted = rates[1:, 0][:, None, None] ** 2 * schur_all[1:]
    following = jnp.concatenate([shifted, jnp.zeros((1, NODES, NODES), jnp.float32)], axis=0)
    separators = lax.map(lambda inputs: assemble(inputs[0], inputs[1]), (coefs[:, 1], grams[:, 1]))
    separator_block = separators - rates[:, 1][:, None, None] ** 2 * schur_all - following
    separator_coupling = -(rates[:, 0] * rates[:, 1])[:, None, None] * schur_all
    return (separator_block, separator_coupling, interior_logdet)
```

```python
import functools
import jax
import jax.numpy as jnp
from jax import lax
from jax.experimental import pallas as pl
from jax.experimental.pallas import tpu as pltpu
from jax.sharding import PartitionSpec as P

def halves(x):
    high = x.astype(jnp.bfloat16)
    return high, (x - high.astype(jnp.float32)).astype(jnp.bfloat16)

def dot3(a, b):
    ah, al = halves(a); bh, bl = halves(b)
    return jnp.dot(jnp.concatenate([ah, al, ah], 1), jnp.concatenate([bh, bh, bl], 0), preferred_element_type=jnp.float32)

def pair_inverse(a, b, d):
    det = a * d - b * b
    r = 1.0 / det
    return d * r, -b * r, a * r, det

def invert_tile(tiles, log_det):
    width = tiles[0].shape[1]
    shape = (8, width)
    lane = lax.broadcasted_iota(jnp.int32, shape, 1)
    sub = lax.broadcasted_iota(jnp.int32, shape, 0)
    for p in range(0, width, 4):
        home, first = p // 8, p % 8
        cols = [[jnp.broadcast_to(t[:, p + j:p + j + 1], shape) for t in tiles] for j in range(4)]
        s = {}
        for j in range(4):
            for i in range(j, 4):
                s[i, j] = jnp.broadcast_to(cols[j][home][first + i:first + i + 1, :], shape)
        a, b, d, det1 = pair_inverse(s[0, 0], s[1, 0], s[1, 1])
        q = [[s[2, 0], s[2, 1]], [s[3, 0], s[3, 1]]]
        m = [[q[i][0] * a + q[i][1] * b, q[i][0] * b + q[i][1] * d] for i in range(2)]
        u = s[2, 2] - (m[0][0] * q[0][0] + m[0][1] * q[0][1])
        v = s[3, 2] - (m[1][0] * q[0][0] + m[1][1] * q[0][1])
        w = s[3, 3] - (m[1][0] * q[1][0] + m[1][1] * q[1][1])
        u, v, w, det2 = pair_inverse(u, v, w)
        log_det = log_det + (jnp.log(det1) + jnp.log(det2))
        lower = [[u * m[0][j] + v * m[1][j] for j in range(2)], [v * m[0][j] + w * m[1][j] for j in range(2)]]
        w00 = a + (m[0][0] * lower[0][0] + m[1][0] * lower[1][0])
        w01 = b + (m[0][0] * lower[0][1] + m[1][0] * lower[1][1])
        w11 = d + (m[0][1] * lower[0][1] + m[1][1] * lower[1][1])
        inv = [[w00, w01, -lower[0][0], -lower[1][0]],
               [w01, w11, -lower[0][1], -lower[1][1]],
               [-lower[0][0], -lower[0][1], u, v],
               [-lower[1][0], -lower[1][1], v, w]]
        here = (lane >= p) & (lane < p + 4)
        rows = []
        for i in range(4):
            row = jnp.broadcast_to(tiles[home][first + i:first + i + 1, :], shape)
            rows.append(jnp.where(here, jnp.where(lane == p + i, 1.0, 0.0), row))
        out = [(inv[i][0] * rows[0] + inv[i][1] * rows[1]) + (inv[i][2] * rows[2] + inv[i][3] * rows[3]) for i in range(4)]
        new = []
        for t, tile in enumerate(tiles):
            kept = jnp.where(here, 0.0, tile)
            kept = kept - ((cols[0][t] * out[0] + cols[1][t] * out[1]) + (cols[2][t] * out[2] + cols[3][t] * out[3]))
            if t == home:
                for i in range(4):
                    kept = jnp.where(sub == first + i, out[i], kept)
            new.append(kept)
        tiles = new
    return tiles, log_det

def invert_body(x_ref, ld_ref, col_ref, row_ref, tile):
    n = x_ref.shape[0]
    ld_ref[...] = jnp.zeros_like(ld_ref)
    def step(k, _):
        at = pl.ds(pl.multiple_of(k * tile, tile), tile)
        tiles = [x_ref[pl.ds(pl.multiple_of(k * tile + 8 * t, 8), 8), at] for t in range(tile // 8)]
        tiles, ld = invert_tile(tiles, ld_ref[...])
        ld_ref[...] = ld
        w = jnp.concatenate(tiles, 0)
        col_ref[...] = x_ref[:, at]
        x_ref[:, at] = jnp.zeros((n, tile), jnp.float32)
        row = dot3(w, x_ref[at, :])
        row_ref[...] = row
        row_ref[:, at] = w
        row = row_ref[...]
        bh, bl = halves(row)
        right = jnp.concatenate([bh, bh, bl], 0)
        for i in range(n // tile):
            rows = slice(i * tile, (i + 1) * tile)
            ah, al = halves(col_ref[rows, :])
            x_ref[rows, :] -= jnp.dot(jnp.concatenate([ah, al, ah], 1), right, preferred_element_type=jnp.float32)
        x_ref[at, :] = row
        return 0
    lax.fori_loop(0, n // tile, step, 0)

def invert_kernel(a_ref, x_ref, ld_ref, col_ref, row_ref, *, tile):
    x_ref[...] = a_ref[...]
    invert_body(x_ref, ld_ref, col_ref, row_ref, tile)

def spd_inverse(a, tile=128):
    n = a.shape[0]
    x, ld = pl.pallas_call(
        functools.partial(invert_kernel, tile=tile),
        out_shape=(jax.ShapeDtypeStruct((n, n), jnp.float32), jax.ShapeDtypeStruct((8, tile), jnp.float32)),
        in_specs=[pl.BlockSpec(memory_space=pltpu.VMEM)],
        out_specs=(pl.BlockSpec(memory_space=pltpu.VMEM),) * 2,
        scratch_shapes=[pltpu.VMEM((n, tile), jnp.float32), pltpu.VMEM((tile, n), jnp.float32)],
        compiler_params=pltpu.CompilerParams(vmem_limit_bytes=40 << 20),
    )(a)
    return x, ld[0, 0]


def order_kernel(step_ref, value_ref, weight_ref, out_ref):
    for k in range(value_ref.shape[0]):
        out_ref[step_ref[k]] = value_ref[k] * jnp.sqrt(weight_ref[k])


def by_step(values, weights, steps):
    return pl.pallas_call(
        order_kernel,
        out_shape=jax.ShapeDtypeStruct(values.shape, jnp.float32),
        in_specs=[
            pl.BlockSpec(memory_space=pltpu.SMEM),
            pl.BlockSpec(memory_space=pltpu.VMEM),
            pl.BlockSpec(memory_space=pltpu.VMEM),
        ],
        out_specs=pl.BlockSpec(memory_space=pltpu.VMEM),
        compiler_params=pltpu.CompilerParams(vmem_limit_bytes=40 << 20),
    )(steps, values, weights[..., None])


def matmul(a, b, contract):
    return lax.dot_general(a, b, (contract, ((), ())), precision=lax.Precision.HIGH)


def scaled_inverse(a):
    scale = lax.rsqrt(jnp.diagonal(a))
    inverse, log_det = spd_inverse(a * scale[:, None] * scale[None, :])
    return inverse, scale, log_det - 2.0 * jnp.sum(jnp.log(scale))


def from_behind(block, axis, distance):
    devices = range(lax.axis_size(axis))
    route = [(i - distance, i) for i in devices if i - distance in devices]
    return lax.ppermute(block, axis, route)


def on_device(prior_space, node_gain, time_diag, rho, obs_values, obs_weight, obs_step):
    size, node_count = prior_space.shape
    part_count = lax.axis_size("tm")
    index_of_tile = lax.axis_index("tile")
    first = index_of_tile == 0
    own_at = index_of_tile * size
    sent = by_step(obs_values[0], obs_weight[0], obs_step[0, 0])
    sent = sent.reshape(part_count, 2, sent.shape[1], size)
    rows = lax.all_to_all(sent, "tm", split_axis=0, concat_axis=0, tiled=True)
    halves_of = [rows[:, s].reshape(-1, size) for s in range(2)]
    prior_own = jnp.where(first, prior_space[:, :size], prior_space[:, size:])
    prior_other = jnp.where(first, prior_space[:, size:], prior_space[:, :size])
    gain_own = jnp.where(first, node_gain[:size], node_gain[size:])
    gain_other = jnp.where(first, node_gain[size:], node_gain[:size])
    diag = time_diag[0] * prior_own + matmul(halves_of[0], halves_of[0], ((0,), (0,)))
    cross = time_diag[0] * prior_other
    inverse, scale, log_first = scaled_inverse(diag)
    panel = scale[:, None] * matmul(inverse, scale[:, None] * cross, ((1,), (0,)))
    swap = [(0, 1), (1, 0)]
    panel_other = lax.ppermute(panel, "tile", swap)
    separator_own = time_diag[1] * prior_own + matmul(halves_of[1], halves_of[1], ((0,), (0,)))
    reduced = diag - matmul(cross, panel_other, ((1,), (0,)))
    inverse, scale, log_second = scaled_inverse(reduced)
    log_other = lax.ppermute(log_first.reshape(1), "tile", swap)
    interior_logdet = (log_second.reshape(1) + log_other) / node_count
    left = gain_own * scale
    schur_own = left[:, None] * inverse * left[None, :]
    schur_other = -left[:, None] * matmul(inverse, scale[:, None] * panel_other.T, ((1,), (0,))) * gain_other[None, :]
    schur_rows = jnp.where(
        first,
        jnp.concatenate([schur_own, schur_other], 1),
        jnp.concatenate([schur_other, schur_own], 1),
    )
    incoming = from_behind(rho[0] * rho[0] * schur_rows, "tm", -1)
    gram = jnp.where(
        first,
        jnp.concatenate([separator_own, time_diag[1] * prior_other], 1),
        jnp.concatenate([time_diag[1] * prior_other, separator_own], 1),
    )
    separator_block = gram - rho[1] * rho[1] * schur_rows - incoming
    separator_coupling = -(rho[0] * rho[1]) * schur_rows
    return (separator_block[None], separator_coupling[None], interior_logdet)


def solution(mesh):
    in_specs = (
        P("tile", None),
        P(),
        P("tm"),
        P("tm"),
        P("tile", "tm", None, None),
        P("tile", "tm", None),
        P("tile", "tm", None),
    )
    out_specs = (P("tm", "tile", None), P("tm", "tile", None), P("tm"))
    return jax.shard_map(
        on_device, mesh=mesh, in_specs=in_specs, out_specs=out_specs, check_vma=False
    )
```

```python
import functools
import jax
import jax.numpy as jnp
from jax import lax
from jax.experimental import pallas as pl
from jax.experimental.pallas import tpu as pltpu
from jax.sharding import PartitionSpec as P

def halves(x):
    high = x.astype(jnp.bfloat16)
    return high, (x - high.astype(jnp.float32)).astype(jnp.bfloat16)

def dot3(a, b):
    ah, al = halves(a); bh, bl = halves(b)
    return jnp.dot(jnp.concatenate([ah, al, ah], 1), jnp.concatenate([bh, bh, bl], 0), preferred_element_type=jnp.float32)

def pair_inverse(a, b, d):
    det = a * d - b * b
    r = 1.0 / det
    return d * r, -b * r, a * r, det

def invert_tile(tiles, log_det):
    width = tiles[0].shape[1]
    shape = (8, width)
    lane = lax.broadcasted_iota(jnp.int32, shape, 1)
    sub = lax.broadcasted_iota(jnp.int32, shape, 0)
    for p in range(0, width, 4):
        home, first = p // 8, p % 8
        cols = [[jnp.broadcast_to(t[:, p + j:p + j + 1], shape) for t in tiles] for j in range(4)]
        s = {}
        for j in range(4):
            for i in range(j, 4):
                s[i, j] = jnp.broadcast_to(cols[j][home][first + i:first + i + 1, :], shape)
        a, b, d, det1 = pair_inverse(s[0, 0], s[1, 0], s[1, 1])
        q = [[s[2, 0], s[2, 1]], [s[3, 0], s[3, 1]]]
        m = [[q[i][0] * a + q[i][1] * b, q[i][0] * b + q[i][1] * d] for i in range(2)]
        u = s[2, 2] - (m[0][0] * q[0][0] + m[0][1] * q[0][1])
        v = s[3, 2] - (m[1][0] * q[0][0] + m[1][1] * q[0][1])
        w = s[3, 3] - (m[1][0] * q[1][0] + m[1][1] * q[1][1])
        u, v, w, det2 = pair_inverse(u, v, w)
        log_det = log_det + (jnp.log(det1) + jnp.log(det2))
        lower = [[u * m[0][j] + v * m[1][j] for j in range(2)], [v * m[0][j] + w * m[1][j] for j in range(2)]]
        w00 = a + (m[0][0] * lower[0][0] + m[1][0] * lower[1][0])
        w01 = b + (m[0][0] * lower[0][1] + m[1][0] * lower[1][1])
        w11 = d + (m[0][1] * lower[0][1] + m[1][1] * lower[1][1])
        inv = [[w00, w01, -lower[0][0], -lower[1][0]],
               [w01, w11, -lower[0][1], -lower[1][1]],
               [-lower[0][0], -lower[0][1], u, v],
               [-lower[1][0], -lower[1][1], v, w]]
        here = (lane >= p) & (lane < p + 4)
        rows = []
        for i in range(4):
            row = jnp.broadcast_to(tiles[home][first + i:first + i + 1, :], shape)
            rows.append(jnp.where(here, jnp.where(lane == p + i, 1.0, 0.0), row))
        out = [(inv[i][0] * rows[0] + inv[i][1] * rows[1]) + (inv[i][2] * rows[2] + inv[i][3] * rows[3]) for i in range(4)]
        new = []
        for t, tile in enumerate(tiles):
            kept = jnp.where(here, 0.0, tile)
            kept = kept - ((cols[0][t] * out[0] + cols[1][t] * out[1]) + (cols[2][t] * out[2] + cols[3][t] * out[3]))
            if t == home:
                for i in range(4):
                    kept = jnp.where(sub == first + i, out[i], kept)
            new.append(kept)
        tiles = new
    return tiles, log_det

def invert_body(x_ref, ld_ref, col_ref, row_ref, tile):
    n = x_ref.shape[0]
    ld_ref[...] = jnp.zeros_like(ld_ref)
    def step(k, _):
        at = pl.ds(pl.multiple_of(k * tile, tile), tile)
        tiles = [x_ref[pl.ds(pl.multiple_of(k * tile + 8 * t, 8), 8), at] for t in range(tile // 8)]
        tiles, ld = invert_tile(tiles, ld_ref[...])
        ld_ref[...] = ld
        w = jnp.concatenate(tiles, 0)
        col_ref[...] = x_ref[:, at]
        x_ref[:, at] = jnp.zeros((n, tile), jnp.float32)
        row = dot3(w, x_ref[at, :])
        row_ref[...] = row
        row_ref[:, at] = w
        row = row_ref[...]
        bh, bl = halves(row)
        right = jnp.concatenate([bh, bh, bl], 0)
        for i in range(n // tile):
            rows = slice(i * tile, (i + 1) * tile)
            ah, al = halves(col_ref[rows, :])
            x_ref[rows, :] -= jnp.dot(jnp.concatenate([ah, al, ah], 1), right, preferred_element_type=jnp.float32)
        x_ref[at, :] = row
        return 0
    lax.fori_loop(0, n // tile, step, 0)

def invert_kernel(a_ref, x_ref, ld_ref, col_ref, row_ref, *, tile):
    x_ref[...] = a_ref[...]
    invert_body(x_ref, ld_ref, col_ref, row_ref, tile)

def spd_inverse(a, tile=128):
    n = a.shape[0]
    x, ld = pl.pallas_call(
        functools.partial(invert_kernel, tile=tile),
        out_shape=(jax.ShapeDtypeStruct((n, n), jnp.float32), jax.ShapeDtypeStruct((8, tile), jnp.float32)),
        in_specs=[pl.BlockSpec(memory_space=pltpu.VMEM)],
        out_specs=(pl.BlockSpec(memory_space=pltpu.VMEM),) * 2,
        scratch_shapes=[pltpu.VMEM((n, tile), jnp.float32), pltpu.VMEM((tile, n), jnp.float32)],
        compiler_params=pltpu.CompilerParams(vmem_limit_bytes=24 << 20),
        cost_estimate=pl.CostEstimate(flops=50 * n**3, bytes_accessed=8 * n * n, transcendentals=0),
    )(a)
    return x, ld[0, 0]


def order_kernel(step_ref, value_ref, weight_ref, out_ref):
    for k in range(value_ref.shape[0]):
        out_ref[step_ref[k]] = value_ref[k] * jnp.sqrt(weight_ref[k])


def by_step(values, weights, steps):
    return pl.pallas_call(
        order_kernel,
        out_shape=jax.ShapeDtypeStruct(values.shape, jnp.float32),
        in_specs=[
            pl.BlockSpec(memory_space=pltpu.SMEM),
            pl.BlockSpec(memory_space=pltpu.VMEM),
            pl.BlockSpec(memory_space=pltpu.VMEM),
        ],
        out_specs=pl.BlockSpec(memory_space=pltpu.VMEM),
        compiler_params=pltpu.CompilerParams(vmem_limit_bytes=40 << 20),
    )(steps, values, weights[..., None])


def matmul(a, b, contract):
    return lax.dot_general(a, b, (contract, ((), ())), precision=lax.Precision.HIGH)


def scaled_inverse(a):
    here = jnp.eye(a.shape[0], dtype=jnp.bool_)
    scale = lax.rsqrt(jnp.sum(jnp.where(here, a, 0.0), 1))
    inverse, log_det = spd_inverse(a * scale[:, None] * scale[None, :])
    return inverse, scale, log_det - 2.0 * jnp.sum(jnp.log(scale))


def from_behind(block, axis, distance):
    devices = range(lax.axis_size(axis))
    route = [(i - distance, i) for i in devices if i - distance in devices]
    return lax.ppermute(block, axis, route)


def pack(symmetric, tile=128):
    count = symmetric.shape[0] // tile
    rows = []
    for r in range(count // 2):
        low, high = (r + 1) * tile, (count - r) * tile
        rows.append(
            jnp.concatenate([symmetric[low - tile : low, :low], symmetric[high - tile : high, :high]], 1)
        )
    return jnp.concatenate(rows, 0)


def unpack(packed, size, tile=128):
    count = size // tile
    rows = [None] * count
    for r in range(count // 2):
        low = (r + 1) * tile
        line = packed[low - tile : low]
        rows[r] = jnp.pad(line[:, :low], ((0, 0), (0, size - low)))
        rows[count - 1 - r] = jnp.pad(line[:, low:], ((0, 0), (0, r * tile)))
    lower = jnp.concatenate(rows, 0)
    block = jnp.arange(size) // tile
    return jnp.where(block[:, None] >= block[None, :], lower, lower.T)


def on_device(prior_space, node_gain, time_diag, rho, obs_values, obs_weight, obs_step):
    size, node_count = prior_space.shape
    part_count = lax.axis_size("tm")
    index_of_tile = lax.axis_index("tile")
    first = index_of_tile == 0
    own_at = index_of_tile * size
    sent = by_step(obs_values[0], obs_weight[0], obs_step[0, 0])
    sent = sent.reshape(part_count, 2, sent.shape[1], size)
    halves_of = [
        lax.all_to_all(sent[:, s], "tm", split_axis=0, concat_axis=0, tiled=True).reshape(-1, size)
        for s in range(2)
    ]
    prior_own = jnp.where(first, prior_space[:, :size], prior_space[:, size:])
    prior_other = jnp.where(first, prior_space[:, size:], prior_space[:, :size])
    gain_own = jnp.where(first, node_gain[:size], node_gain[size:])
    gain_other = jnp.where(first, node_gain[size:], node_gain[:size])
    diag = time_diag[0] * prior_own + matmul(halves_of[0], halves_of[0], ((0,), (0,)))
    cross = time_diag[0] * prior_other
    inverse, scale, log_first = scaled_inverse(diag)
    panel = scale[:, None] * matmul(inverse, scale[:, None] * cross, ((1,), (0,)))
    swap = [(0, 1), (1, 0)]
    panel_other = lax.ppermute(panel, "tile", swap)
    separator_own = time_diag[1] * prior_own + matmul(halves_of[1], halves_of[1], ((0,), (0,)))
    reduced = diag - matmul(cross, panel_other, ((1,), (0,)))
    inverse, scale, log_second = scaled_inverse(reduced)
    log_other = lax.ppermute(log_first.reshape(1), "tile", swap)
    interior_logdet = (log_second.reshape(1) + log_other) / node_count
    left = gain_own * scale
    schur_own = left[:, None] * inverse * left[None, :]
    schur_other = -left[:, None] * matmul(inverse, scale[:, None] * panel_other.T, ((1,), (0,))) * gain_other[None, :]
    decay = rho[0] * rho[0]
    half = size // 2
    own_next = unpack(from_behind(decay * pack(schur_own), "tm", -1), size)
    sent_half = decay * jnp.where(first, schur_other[:half], schur_other[:, half:].T)
    half_next = from_behind(sent_half, "tm", -1)
    half_swapped = lax.ppermute(half_next, "tile", swap)
    other_next = jnp.where(
        first,
        jnp.concatenate([half_next, half_swapped], 0),
        jnp.concatenate([half_swapped, half_next], 0).T,
    )

    def in_order(own, other):
        return jnp.where(
            first, jnp.concatenate([own, other], 1), jnp.concatenate([other, own], 1)
        )

    schur_rows = in_order(schur_own, schur_other)
    incoming = in_order(own_next, other_next)
    gram = in_order(separator_own, time_diag[1] * prior_other)
    separator_block = gram - rho[1] * rho[1] * schur_rows - incoming
    separator_coupling = -(rho[0] * rho[1]) * schur_rows
    return (separator_block[None], separator_coupling[None], interior_logdet)


def solution(mesh):
    in_specs = (
        P("tile", None),
        P(),
        P("tm"),
        P("tm"),
        P("tile", "tm", None, None),
        P("tile", "tm", None),
        P("tile", "tm", None),
    )
    out_specs = (P("tm", "tile", None), P("tm", "tile", None), P("tm"))
    return jax.shard_map(
        on_device, mesh=mesh, in_specs=in_specs, out_specs=out_specs, check_vma=False
    )
```
